512 devices in a mesh: energy: 32 (over y, z_lo, core), slab: 16 (over x, z_hi).
Axes of the slice: x: 4, y: 8, z: 8 (z_hi: 4, z_lo: 2; z = z_hi * 2 + z_lo), core: 2. Of those that a mesh axis runs over, the one named last changes fastest.
Arguments:
- green_lesser: float32 [64, 16, 2, 128, 128], P('energy', 'slab'), may hold values from -6 to 6
- coupling: float32 [4, 16, 3, 2, 128, 128], P(None, 'slab'), may hold values from -0.375 to 0.375
- occupation: float32 [4], replicated, may hold values from 0.2 to 3
- shifts: int32 [4], replicated, may hold values from 1 to 2, as said below
- neighbours: int32 [16, 3], P('slab'), may hold values from 0 to 15, as said below
Outputs:
- self_energy: float32 [64, 16, 2, 128, 128], P('energy', 'slab')
The draws below stay inside these ranges and needn't reach their ends.
Inputs may be any that keep to these rules, and one draw needn't show every extreme that they name: `shifts`: some mode's shift is 1 and some mode's shift is 2. `neighbours`: entry 0 of row i is max(i - 1, 0), entry 2 is min(i + 1, 15), entry 1 lies within one of i.
All inputs are finite; a program needn't handle non-finite values.
Results may differ from the reference program's by a relative error of at most 0.0001.
Values sent between devices are 32-bit elements; how exact they have to be, the bound alone decides.
A program may use at most 64 MiB of HBM per device.

```python
import math
import jax
import jax.numpy as jnp
from jax import lax

E_DEV = 2
MODES = 4
K = 3
BLK = 128
NE = 64
NB = 16


def draw_shifts(key, part):
    base = jax.random.randint(key, (MODES,), 1, E_DEV + 1)
    order_modes = jax.random.permutation(jax.random.fold_in(key, 7), MODES)
    modes = jnp.arange(MODES)
    base = jnp.where(modes == order_modes[0], 1, base)
    base = jnp.where(modes == order_modes[1], E_DEV, base)
    return base.astype(jnp.int32)


def draw_neighbours(key, part):
    middle = jax.random.randint(key, (NB,), -1, 2)
    rows = jnp.arange(NB)
    offsets = jnp.stack([-jnp.ones_like(middle), middle, jnp.ones_like(middle)], axis=1)
    return jnp.clip(rows[:, None] + offsets, 0, NB - 1).astype(jnp.int32)


def block_scale(own_key, dims, split, low, top_value):
    def one(position, shards_of):
        steps = jax.random.uniform(jax.random.fold_in(jax.random.fold_in(own_key, 6), position), (shards_of,), jnp.float32, low / len(split), top_value / len(split))
        return jnp.repeat(jnp.exp(steps), dims[position] // shards_of).reshape((-1,) + (1,) * (len(dims) - position - 1))

    level = one(*split[0])
    for cut in split[1:]:
        level = level * one(*cut)
    return level


def bell_draw(key, dims, scale, most, cuts=(), kind=jnp.bfloat16):
    loudness = block_scale(key, dims, cuts, -0.22, 0.18) if cuts else 1.0
    drawn = jax.random.normal(key, dims, jnp.float32) * scale * loudness
    return jnp.minimum(jnp.maximum(drawn, -most), most).astype(kind)


def setup_inputs(seed: int = 0) -> dict:
    key_list = jax.random.split(jax.random.key(seed), 6)
    return {
        "green_lesser": bell_draw(key_list[0], (NE, NB, 2, BLK, BLK), 1.0, 6.0, ((0, 32), (1, 16)), jnp.float32),
        "coupling": bell_draw(key_list[1], (MODES, NB, K, 2, BLK, BLK), (2 * BLK) ** -0.5, 0.375, ((1, 16),), jnp.float32),
        "occupation": jnp.clip(jnp.exp(jax.random.uniform(key_list[2], (MODES,), jnp.float32, math.log(0.2), math.log(3.0))), 0.2, 3.0),
        "shifts": draw_shifts(jax.random.fold_in(key_list[5], 71), 0),
        "neighbours": draw_neighbours(jax.random.fold_in(key_list[5], 71), 0),
    }


def precise_matmul(first, second):
    return jnp.matmul(first, second, precision=lax.Precision.HIGHEST)


def complex_product(leading, trailing):
    lead_real, lead_imag = leading[..., 0, :, :], leading[..., 1, :, :]
    trail_real, trail_imag = trailing[..., 0, :, :], trailing[..., 1, :, :]
    real_part = precise_matmul(lead_real, trail_real) - precise_matmul(lead_imag, trail_imag)
    imag_part = precise_matmul(lead_real, trail_imag) + precise_matmul(lead_imag, trail_real)
    return jnp.stack([real_part, imag_part], axis=-3)


def adjoint_product(leading, trailing):
    lead_real, lead_imag = leading[..., 0, :, :], leading[..., 1, :, :]
    trail_real = jnp.swapaxes(trailing[..., 0, :, :], -1, -2)
    trail_imag = jnp.swapaxes(trailing[..., 1, :, :], -1, -2)
    real_part = precise_matmul(lead_real, trail_real) + precise_matmul(lead_imag, trail_imag)
    imag_part = precise_matmul(lead_imag, trail_real) - precise_matmul(lead_real, trail_imag)
    return jnp.stack([real_part, imag_part], axis=-3)


def sandwich(couple, middle):
    return adjoint_product(complex_product(couple, middle), couple)


def reference(green_lesser, coupling, occupation, shifts, neighbours):
    padded = jnp.pad(green_lesser, ((E_DEV, E_DEV), (0, 0), (0, 0), (0, 0), (0, 0)))

    def one_energy(energy):
        summed = jnp.zeros((NB, 2, BLK, BLK), jnp.float32)
        for mode_index in range(MODES):
            shift_now = shifts[mode_index]
            upper_green = lax.dynamic_index_in_dim(padded, energy + E_DEV + shift_now, 0, keepdims=False)
            lower_green = lax.dynamic_index_in_dim(padded, energy + E_DEV - shift_now, 0, keepdims=False)
            weighted = (occupation[mode_index] + 1.0) * upper_green[neighbours] + occupation[mode_index] * lower_green[neighbours]
            summed = summed + jnp.sum(sandwich(coupling[mode_index], weighted), axis=1)
        return summed

    return lax.map(one_energy, jnp.arange(NE, dtype=jnp.int32))
```

```python
import functools

import jax
import jax.numpy as jnp
from jax import lax
from jax.experimental import pallas as pl
from jax.experimental.pallas import tpu as pltpu
from jax.sharding import PartitionSpec as P

MESH = pl.DeviceIdType.MESH
CHUNKS = 4
AHEAD = 2
OWN = 1


def halves(value):
    high = value.astype(jnp.bfloat16)
    return high, (value - high.astype(jnp.float32)).astype(jnp.bfloat16)


def kernel(energy_count, energies, slabs, occ_ref, shift_ref, near_ref, g_ref, c_ref, out_ref, *scratch):
    bufs = scratch[:CHUNKS]
    couple, adjoint_high, adjoint_low, left = scratch[CHUNKS : CHUNKS + 4]
    middle_high, middle_low, total = scratch[CHUNKS + 4 : CHUNKS + 7]
    send_sem, recv_sem, own_sem, couple_sem, ready_sem = scratch[CHUNKS + 7 :]
    modes, ks = c_ref.shape[0], c_ref.shape[2]
    size = c_ref.shape[-1]
    rows = size // CHUNKS

    a, s = lax.axis_index("energy"), lax.axis_index("slab")
    core, layer = lax.rem(a, 2), lax.rem(lax.div(a, 2), 2)
    step = 2 * core - 1

    def ring(value, count):
        return lax.rem(value + count, count)

    outer, partner = ring(a + step, energies), ring(a - step, energies)
    across = jnp.where(layer == 0, s - 1, s + 1)
    close = 2 - 2 * layer
    far = 2 * layer
    has_far = (across >= 0) & (across < slabs)
    has_close = (2 * s - across >= 0) & (2 * s - across < slabs)

    def own_block(r):
        return g_ref.at[:, 0, :, pl.ds(r * rows, rows), :]

    def slot(r, side, place):
        return bufs[r].at[side, pl.ds(2 * place, 2)]

    def remote(flow, r, source, side, place, target):
        return pltpu.make_async_remote_copy(
            src_ref=source,
            dst_ref=slot(r, side, place),
            send_sem=send_sem.at[flow, r],
            recv_sem=recv_sem.at[r, side, place],
            device_id={"energy": target[0], "slab": target[1]},
            device_id_type=MESH,
        )

    def flow_copy(flow, r):
        own = own_block(r)
        table = (
            (own, OWN, 1 - step, (outer, s)),
            (own, OWN, 1 + step, (partner, s)),
            (own, close, 1 - step, (outer, across)),
            (slot(r, OWN, 1 + step), close, 1, (outer, across)),
            (slot(r, far, 1 + step), far, 1, (outer, s)),
            (slot(r, far, 1), far, 1 - step, (outer, s)),
            (slot(r, far, 1), far, 1 + step, (partner, s)),
            (slot(r, close, 1), close, 1 + step, (partner, s)),
        )
        return remote(flow, r, *table[flow])

    def arrived(r, side, place):
        remote(0, r, slot(r, side, place), side, place, (outer, s)).wait_recv()

    couple_copy = pltpu.make_async_copy(c_ref, couple, couple_sem)
    couple_copy.start()

    def signal(semaphore, target):
        pl.semaphore_signal(
            semaphore, inc=1, device_id={"energy": target[0], "slab": target[1]}, device_id_type=MESH
        )

    barrier = pltpu.get_barrier_semaphore()
    signal(barrier, (outer, s))
    signal(barrier, (partner, s))

    @pl.when((layer == 0) & has_far)
    def _():
        signal(barrier, (outer, across))

    own_copies = [
        pltpu.make_async_copy(own_block(r), slot(r, OWN, 1), own_sem.at[r]) for r in range(CHUNKS)
    ]
    for copy in own_copies:
        copy.start()
    pl.semaphore_wait(barrier, jnp.where((layer == 1) & has_far, 3, 2))

    @pl.when((layer == 1) & has_far)
    def _():
        signal(ready_sem, (outer, across))
        for r in range(AHEAD):
            flow_copy(2, r).start()

    for r in range(CHUNKS):
        flow_copy(0, r).start()
        flow_copy(1, r).start()

    def prepare():
        couple_copy.wait()

        def mode_step(m, _):
            for k in range(ks):
                real, imag = couple[m, 0, k, 0], couple[m, 0, k, 1]
                real_t, imag_t = real.T, imag.T
                adjoint = jnp.concatenate(
                    [
                        jnp.concatenate([real_t, -imag_t], axis=1),
                        jnp.concatenate([imag_t, real_t], axis=1),
                    ],
                    axis=0,
                )
                high, low = halves(adjoint)
                adjoint_high[m, k] = high
                adjoint_low[m, k] = low
            return 0

        lax.fori_loop(0, modes, mode_step, 0)
        for r in range(CHUNKS):
            for k in range(ks):
                stacked = jnp.concatenate(
                    [
                        couple[m, 0, k, part][:, r * rows : (r + 1) * rows]
                        for m in range(modes)
                        for part in range(2)
                    ],
                    axis=1,
                )
                high, low = halves(stacked)
                left[r, k, :size] = high
                left[r, k, size:] = low

    def relay_far(r):
        arrived(r, OWN, 1 + step)

        @pl.when(has_far)
        def _():
            flow_copy(3, r).start()
            if r + AHEAD < CHUNKS:
                flow_copy(2, r + AHEAD).start()
            arrived(r, far, 1 + step)
            flow_copy(4, r).start()

    def relay_close(r):
        @pl.when(has_far)
        def _():
            arrived(r, far, 1)
            flow_copy(5, r).start()
            flow_copy(6, r).start()

        @pl.when(has_close)
        def _():
            arrived(r, close, 1)
            flow_copy(7, r).start()

    first_energy = a * energy_count
    top = energies * energy_count

    def stage(r):
        arrived(r, OWN, 1 - step)

        @pl.when(has_far)
        def _():
            arrived(r, far, 1 - step)

        @pl.when(has_close)
        def _():
            arrived(r, close, 0)
            arrived(r, close, 2)

        own_copies[r].wait()
        buf = bufs[r]
        span = modes * 2 * rows

        def k_step(k, _):
            place = jnp.clip(near_ref[0, k] - s + 1, 0, 2)
            for m in range(modes):
                shift = shift_ref[m]
                count = occ_ref[m]
                pieces = []
                for e in range(energy_count):
                    energy = first_energy + e
                    more = jnp.where(energy + shift < top, count + 1.0, 0.0)
                    less = jnp.where(energy - shift >= 0, count, 0.0)
                    above, below = energy_count + e + shift, energy_count + e - shift
                    pieces.append(
                        jnp.concatenate(
                            [
                                more * buf[place, above, part] + less * buf[place, below, part]
                                for part in range(2)
                            ],
                            axis=1,
                        )
                    )
                high, low = halves(jnp.concatenate(pieces, axis=0))
                count_rows = energy_count * rows
                first = jnp.dot(
                    jnp.concatenate([high, low], axis=0),
                    adjoint_high[m, k],
                    preferred_element_type=jnp.float32,
                )
                second = jnp.dot(high, adjoint_low[m, k], preferred_element_type=jnp.float32)
                result = first[:count_rows] + first[count_rows:] + second
                for e in range(energy_count):
                    part = result[e * rows : (e + 1) * rows]
                    turned = jnp.concatenate([-part[:, size:], part[:, :size]], axis=1)
                    base = m * 2 * rows
                    columns = slice(e * 2 * size, (e + 1) * 2 * size)
                    for offset, value in ((0, part), (rows, turned)):
                        high_value, low_value = halves(value)
                        middle_high[base + offset : base + offset + rows, columns] = high_value
                        middle_low[base + offset : base + offset + rows, columns] = low_value
            lhs = left[r, k]
            both = jnp.dot(lhs, middle_high[...], preferred_element_type=jnp.float32)
            rest = jnp.dot(lhs[:size], middle_low[...], preferred_element_type=jnp.float32)
            total[...] += both[:size] + both[size:] + rest
            return 0

        lax.fori_loop(0, ks, k_step, 0)

    total[...] = jnp.zeros_like(total)
    prepare()

    @pl.when((layer == 0) & has_far)
    def _():
        pl.semaphore_wait(ready_sem, 1)
        for r in range(AHEAD):
            flow_copy(2, r).start()

    for r in range(CHUNKS):
        relay_far(r)
        if r >= 1:
            relay_close(r - 1)
        if r >= 2:
            stage(r - 2)
    relay_close(CHUNKS - 1)
    stage(CHUNKS - 2)
    stage(CHUNKS - 1)
    for e in range(energy_count):
        for part in range(2):
            start = (2 * e + part) * size
            out_ref[e, 0, part] = total[:, start : start + size]
    for r in range(CHUNKS):
        for flow in (0, 1):
            flow_copy(flow, r).wait_send()

        @pl.when(has_far)
        def _():
            for flow in range(2, 7):
                flow_copy(flow, r).wait_send()

        @pl.when(has_close)
        def _():
            flow_copy(7, r).wait_send()


def solution(mesh):
    energies, slabs = mesh.shape["energy"], mesh.shape["slab"]

    def shards(green_lesser, coupling, occupation, shifts, neighbours):
        energy_count, _, _, size, _ = green_lesser.shape
        modes, _, ks = coupling.shape[:3]
        rows = size // CHUNKS
        bf16, f32 = jnp.bfloat16, jnp.float32
        smem = pl.BlockSpec(memory_space=pltpu.SMEM)
        hbm = pl.BlockSpec(memory_space=pl.ANY)
        return pl.pallas_call(
            functools.partial(kernel, energy_count, energies, slabs),
            out_shape=jax.ShapeDtypeStruct(green_lesser.shape, f32),
            in_specs=[smem, smem, smem, hbm, hbm],
            out_specs=pl.BlockSpec(memory_space=pltpu.VMEM),
            scratch_shapes=[pltpu.VMEM((3, 3 * energy_count, 2, rows, size), f32) for _ in range(CHUNKS)]
            + [
                pltpu.VMEM(coupling.shape, f32),
                pltpu.VMEM((modes, ks, 2 * size, 2 * size), bf16),
                pltpu.VMEM((modes, ks, 2 * size, 2 * size), bf16),
                pltpu.VMEM((CHUNKS, ks, 2 * size, modes * 2 * rows), bf16),
                pltpu.VMEM((modes * 2 * rows, energy_count * 2 * size), bf16),
                pltpu.VMEM((modes * 2 * rows, energy_count * 2 * size), bf16),
                pltpu.VMEM((size, energy_count * 2 * size), f32),
                pltpu.SemaphoreType.DMA((8, CHUNKS)),
                pltpu.SemaphoreType.DMA((CHUNKS, 3, 3)),
                pltpu.SemaphoreType.DMA((CHUNKS,)),
                pltpu.SemaphoreType.DMA,
                pltpu.SemaphoreType.REGULAR,
            ],
            compiler_params=pltpu.CompilerParams(collective_id=0, has_side_effects=True),
        )(occupation, shifts, neighbours, green_lesser, coupling)

    return jax.shard_map(
        shards,
        mesh=mesh,
        in_specs=(
            P("energy", "slab", None, None, None),
            P(None, "slab", None, None, None, None),
            P(),
            P(),
            P("slab", None),
        ),
        out_specs=P("energy", "slab", None, None, None),
        check_vma=False,
    )
```

```python
import functools

import jax
import jax.numpy as jnp
from jax import lax
from jax.experimental import pallas as pl
from jax.experimental.pallas import tpu as pltpu
from jax.sharding import PartitionSpec as P

MESH = pl.DeviceIdType.MESH
ROWS = (64, 64)
STARTS = tuple(sum(ROWS[:r]) for r in range(len(ROWS)))
CHUNKS = len(ROWS)
AHEAD = 2
LAG = 2
OWN = 1
SPARE = 3


def halves(value):
    high = value.astype(jnp.bfloat16)
    return high, (value - high.astype(jnp.float32)).astype(jnp.bfloat16)


def kernel(energy_count, energies, slabs, occ_ref, shift_ref, near_ref, g_ref, c_ref, out_ref, *scratch):
    bufs, scratch = scratch[:CHUNKS], scratch[CHUNKS:]
    lefts, scratch = scratch[:CHUNKS], scratch[CHUNKS:]
    couple, adjoint_high, adjoint_low, middle_high, middle_low, total = scratch[:6]
    send_sem, recv_sem, own_sem, couple_sem, ready_sem = scratch[6:]
    modes, ks, size = c_ref.shape[0], c_ref.shape[2], c_ref.shape[-1]

    a, s = lax.axis_index("energy"), lax.axis_index("slab")
    core, layer = lax.rem(a, 2), lax.rem(lax.div(a, 2), 2)
    step = 2 * core - 1
    partner = a - step
    mate = a + 3 - 2 * lax.rem(a, 4)
    edge = core == layer
    onto, behind = a - 4 * step, a + 4 * step
    has_onto = edge & (onto >= 0) & (onto < energies)
    has_behind = edge & (behind >= 0) & (behind < energies)
    beside = a + step
    has_beside = (beside >= 0) & (beside < energies)
    across = jnp.where(layer == 0, s - 1, s + 1)
    opposite = 2 * s - across
    close = 2 - 2 * layer
    far = 2 * layer
    has_far = (across >= 0) & (across < slabs)
    has_close = (opposite >= 0) & (opposite < slabs)
    inner, outer = 1 - step, 1 + step
    mine, theirs = jnp.where(edge, SPARE, outer), jnp.where(edge, SPARE, inner)

    def own_block(r):
        return g_ref.at[:, 0, :, pl.ds(STARTS[r], ROWS[r]), :]

    def slot(r, side, place):
        return bufs[r].at[side, pl.ds(energy_count * place, energy_count)]

    def remote(flow, r, source, side, place, target):
        return pltpu.make_async_remote_copy(
            src_ref=source,
            dst_ref=slot(r, side, place),
            send_sem=send_sem.at[flow, r],
            recv_sem=recv_sem.at[r, side, place],
            device_id={"energy": target[0], "slab": target[1]},
            device_id_type=MESH,
        )

    def flow_copy(flow, r):
        own = own_block(r)
        table = (
            (own, OWN, theirs, (mate, s)),
            (own, OWN, outer, (partner, s)),
            (own, close, theirs, (mate, across)),
            (slot(r, OWN, mine), close, 1, (mate, across)),
            (slot(r, far, mine), far, 1, (mate, s)),
            (slot(r, far, 1), far, inner, (beside, s)),
            (slot(r, far, 1), far, outer, (partner, s)),
            (slot(r, close, 1), close, outer, (partner, s)),
            (slot(r, OWN, SPARE), OWN, outer, (onto, s)),
            (slot(r, far, SPARE), far, outer, (onto, s)),
        )
        return remote(flow, r, *table[flow])

    def send(flow, r):
        flow_copy(flow, r).start()

    def arrived(r, side, place):
        remote(0, r, slot(r, side, place), side, place, (mate, s)).wait_recv()

    def signal(semaphore, target):
        pl.semaphore_signal(
            semaphore, inc=1, device_id={"energy": target[0], "slab": target[1]}, device_id_type=MESH
        )

    barrier = pltpu.get_barrier_semaphore()
    signal(barrier, (mate, s))
    signal(barrier, (partner, s))

    @pl.when((layer == 0) & has_far)
    def _():
        signal(barrier, (mate, across))

    @pl.when(has_onto)
    def _():
        signal(barrier, (onto, s))

    @pl.when(has_behind)
    def _():
        signal(barrier, (behind, s))
        signal(barrier, (beside, s))

    couple_copy = pltpu.make_async_copy(c_ref, couple, couple_sem)
    couple_copy.start()
    own_copies = [
        pltpu.make_async_copy(own_block(r), slot(r, OWN, 1), own_sem.at[r]) for r in range(CHUNKS)
    ]
    for copy in own_copies:
        copy.start()
    pl.semaphore_wait(
        barrier,
        2
        + ((layer == 1) & has_far).astype(jnp.int32)
        + has_onto.astype(jnp.int32)
        + 2 * has_behind.astype(jnp.int32),
    )

    @pl.when((layer == 1) & has_far)
    def _():
        signal(ready_sem, (mate, across))
        for r in range(AHEAD):
            send(2, r)

    for r in range(CHUNKS):
        send(0, r)
        send(1, r)

    def prepare():
        couple_copy.wait()

        def mode_step(m, _):
            for k in range(ks):
                real_t, imag_t = couple[m, 0, k, 0].T, couple[m, 0, k, 1].T
                adjoint = jnp.concatenate(
                    [
                        jnp.concatenate([real_t, -imag_t], axis=1),
                        jnp.concatenate([imag_t, real_t], axis=1),
                    ],
                    axis=0,
                )
                adjoint_high[m, k], adjoint_low[m, k] = halves(adjoint)
            return 0

        lax.fori_loop(0, modes, mode_step, 0)
        for r in range(CHUNKS):
            for k in range(ks):
                stacked = jnp.concatenate(
                    [
                        couple[m, 0, k, part][:, STARTS[r] : STARTS[r] + ROWS[r]]
                        for m in range(modes)
                        for part in range(2)
                    ],
                    axis=1,
                )
                high, low = halves(stacked)
                lefts[r][k, :size] = high
                lefts[r][k, size:] = low

    def pass_own(r):
        arrived(r, OWN, mine)

        @pl.when(has_far)
        def _():
            send(3, r)
            if r + AHEAD < CHUNKS:
                send(2, r + AHEAD)

        @pl.when(has_onto)
        def _():
            send(8, r)

    def pass_mates(r):
        @pl.when(has_far)
        def _():
            arrived(r, far, mine)
            send(4, r)

        @pl.when(has_far & has_onto)
        def _():
            send(9, r)

    def pass_far(r):
        @pl.when(has_far)
        def _():
            arrived(r, far, 1)
            send(6, r)

        @pl.when(has_far & has_beside)
        def _():
            send(5, r)

    def pass_close(r):
        @pl.when(has_close)
        def _():
            arrived(r, close, 1)
            send(7, r)

    def gather(r):
        own_copies[r].wait()
        arrived(r, OWN, inner)

        @pl.when(has_behind)
        def _():
            arrived(r, OWN, outer)

        @pl.when(has_far)
        def _():
            arrived(r, far, inner)

        @pl.when(has_far & has_behind)
        def _():
            arrived(r, far, outer)

        @pl.when(has_close)
        def _():
            arrived(r, close, inner)

        @pl.when(has_close & has_beside)
        def _():
            arrived(r, close, outer)

    first_energy = a * energy_count
    top = energies * energy_count

    def multiply(r, low_k, high_k):
        buf, rows = bufs[r], ROWS[r]
        span = modes * 2 * rows

        def k_step(k, _):
            place = jnp.clip(near_ref[0, k] - s + 1, 0, 2)
            for m in range(modes):
                shift = shift_ref[m]
                count = occ_ref[m]
                pieces = []
                for e in range(energy_count):
                    energy = first_energy + e
                    more = jnp.where(energy + shift < top, count + 1.0, 0.0)
                    less = jnp.where(energy - shift >= 0, count, 0.0)
                    above, below = energy_count + e + shift, energy_count + e - shift
                    pieces.append(
                        jnp.concatenate(
                            [
                                more * buf[place, above, part] + less * buf[place, below, part]
                                for part in range(2)
                            ],
                            axis=1,
                        )
                    )
                high, low = halves(jnp.concatenate(pieces, axis=0))
                count_rows = energy_count * rows
                first = jnp.dot(
                    jnp.concatenate([high, low], axis=0),
                    adjoint_high[m, k],
                    preferred_element_type=jnp.float32,
                )
                second = jnp.dot(high, adjoint_low[m, k], preferred_element_type=jnp.float32)
                result = first[:count_rows] + first[count_rows:] + second
                for e in range(energy_count):
                    part = result[e * rows : (e + 1) * rows]
                    turned = jnp.concatenate([-part[:, size:], part[:, :size]], axis=1)
                    base = m * 2 * rows
                    columns = slice(e * 2 * size, (e + 1) * 2 * size)
                    for offset, value in ((0, part), (rows, turned)):
                        high_value, low_value = halves(value)
                        middle_high[base + offset : base + offset + rows, columns] = high_value
                        middle_low[base + offset : base + offset + rows, columns] = low_value
            lhs = lefts[r][k]
            both = jnp.dot(lhs, middle_high[:span], preferred_element_type=jnp.float32)
            rest = jnp.dot(lhs[:size], middle_low[:span], preferred_element_type=jnp.float32)
            total[...] += both[:size] + both[size:] + rest
            return 0

        lax.fori_loop(low_k, high_k, k_step, 0)

    prepare()
    total[...] = jnp.zeros_like(total)

    @pl.when(edge & ~has_behind)
    def _():
        for r in range(CHUNKS):
            for side in range(3):
                for e in range(energy_count):
                    bufs[r][side, energy_count * outer + e] = jnp.zeros((2, ROWS[r], size), jnp.float32)

    @pl.when((layer == 0) & has_far)
    def _():
        pl.semaphore_wait(ready_sem, 1)
        for r in range(AHEAD):
            send(2, r)

    for r in range(CHUNKS):
        pass_own(r)
    for r in range(CHUNKS):
        pass_mates(r)
    for r in range(CHUNKS + LAG):
        if r < CHUNKS:
            pass_far(r)
            pass_close(r)
        if r >= LAG:
            gather(r - LAG)
            multiply(r - LAG, 0, ks)
    for e in range(energy_count):
        for part in range(2):
            start = (2 * e + part) * size
            out_ref[e, 0, part] = total[:, start : start + size]

    for r in range(CHUNKS):
        for flows, sent in (
            ((0, 1), None),
            ((2, 3, 4, 6), has_far),
            ((5,), has_far & has_beside),
            ((7,), has_close),
            ((8,), has_onto),
            ((9,), has_far & has_onto),
        ):

            def finish(flows=flows, r=r):
                for flow in flows:
                    flow_copy(flow, r).wait_send()

            if sent is None:
                finish()
            else:
                pl.when(sent)(finish)


def solution(mesh):
    energies, slabs = mesh.shape["energy"], mesh.shape["slab"]

    def shards(green_lesser, coupling, occupation, shifts, neighbours):
        energy_count, _, _, size, _ = green_lesser.shape
        modes, _, ks = coupling.shape[:3]
        bf16, f32 = jnp.bfloat16, jnp.float32
        smem = pl.BlockSpec(memory_space=pltpu.SMEM)
        hbm = pl.BlockSpec(memory_space=pl.ANY)
        depth = modes * 2 * max(ROWS)
        return pl.pallas_call(
            functools.partial(kernel, energy_count, energies, slabs),
            out_shape=jax.ShapeDtypeStruct(green_lesser.shape, f32),
            in_specs=[smem, smem, smem, hbm, hbm],
            out_specs=pl.BlockSpec(memory_space=pltpu.VMEM),
            scratch_shapes=[pltpu.VMEM((3, 4 * energy_count, 2, rows, size), f32) for rows in ROWS]
            + [pltpu.VMEM((ks, 2 * size, modes * 2 * rows), bf16) for rows in ROWS]
            + [
                pltpu.VMEM(coupling.shape, f32),
                pltpu.VMEM((modes, ks, 2 * size, 2 * size), bf16),
                pltpu.VMEM((modes, ks, 2 * size, 2 * size), bf16),
                pltpu.VMEM((depth, energy_count * 2 * size), bf16),
                pltpu.VMEM((depth, energy_count * 2 * size), bf16),
                pltpu.VMEM((size, energy_count * 2 * size), f32),
                pltpu.SemaphoreType.DMA((10, CHUNKS)),
                pltpu.SemaphoreType.DMA((CHUNKS, 3, 4)),
                pltpu.SemaphoreType.DMA((CHUNKS,)),
                pltpu.SemaphoreType.DMA,
                pltpu.SemaphoreType.REGULAR,
            ],
            compiler_params=pltpu.CompilerParams(collective_id=0, has_side_effects=True),
        )(occupation, shifts, neighbours, green_lesser, coupling)

    return jax.shard_map(
        shards,
        mesh=mesh,
        in_specs=(
            P("energy", "slab", None, None, None),
            P(None, "slab", None, None, None, None),
            P(),
            P(),
            P("slab", None),
        ),
        out_specs=P("energy", "slab", None, None, None),
        check_vma=False,
    )
```

```python
import functools

import jax
import jax.numpy as jnp
from jax import lax
from jax.experimental import pallas as pl
from jax.experimental.pallas import tpu as pltpu
from jax.sharding import PartitionSpec as P

MESH = pl.DeviceIdType.MESH
ROWS = (32, 32, 32, 32)
STARTS = tuple(sum(ROWS[:r]) for r in range(len(ROWS)))
CHUNKS = len(ROWS)
AHEAD = 4
GROUPS = ((0, 1), (2, 3))
OWN = 1
SPARE = 3


def halves(value):
    high = value.astype(jnp.bfloat16)
    return high, (value - high.astype(jnp.float32)).astype(jnp.bfloat16)


def kernel(energy_count, energies, slabs, occ_hbm, shift_hbm, near_hbm, g_ref, c_ref, out_ref, *scratch):
    bufs, scratch = scratch[:CHUNKS], scratch[CHUNKS:]
    lefts, scratch = scratch[: len(GROUPS)], scratch[len(GROUPS) :]
    couple, adjoint_high, adjoint_low, middle_high, middle_low, total = scratch[:6]
    occ_ref, shift_ref, near_ref = scratch[6:9]
    send_sem, recv_sem, own_sem, couple_sem, scalar_sem, ready_sem, go_sem = scratch[9:]
    modes, ks, size = c_ref.shape[0], c_ref.shape[2], c_ref.shape[-1]

    a, s = lax.axis_index("energy"), lax.axis_index("slab")
    core, layer = lax.rem(a, 2), lax.rem(lax.div(a, 2), 2)
    step = 2 * core - 1
    partner = a - step
    mate = a + 3 - 2 * lax.rem(a, 4)
    edge = core == layer
    onto, behind = a - 4 * step, a + 4 * step
    has_onto = edge & (onto >= 0) & (onto < energies)
    has_behind = edge & (behind >= 0) & (behind < energies)
    beside = a + step
    has_beside = (beside >= 0) & (beside < energies)
    across = jnp.where(layer == 0, s - 1, s + 1)
    opposite = 2 * s - across
    close = 2 - 2 * layer
    far = 2 * layer
    has_far = (across >= 0) & (across < slabs)
    has_close = (opposite >= 0) & (opposite < slabs)
    inner, outer = 1 - step, 1 + step
    mine, theirs = jnp.where(edge, SPARE, outer), jnp.where(edge, SPARE, inner)

    def own_block(r):
        return g_ref.at[:, 0, :, pl.ds(STARTS[r], ROWS[r]), :]

    def slot(r, side, place):
        return bufs[r].at[side, pl.ds(energy_count * place, energy_count)]

    def remote(flow, r, source, side, place, target):
        return pltpu.make_async_remote_copy(
            src_ref=source,
            dst_ref=slot(r, side, place),
            send_sem=send_sem.at[flow, r],
            recv_sem=recv_sem.at[r, side, place],
            device_id={"energy": target[0], "slab": target[1]},
            device_id_type=MESH,
        )

    def flow_copy(flow, r):
        own = own_block(r)
        table = (
            (own, OWN, theirs, (mate, s)),
            (own, OWN, outer, (partner, s)),
            (own, close, theirs, (mate, across)),
            (slot(r, OWN, mine), close, 1, (mate, across)),
            (slot(r, far, mine), far, 1, (mate, s)),
            (slot(r, far, 1), far, inner, (beside, s)),
            (slot(r, far, 1), far, outer, (partner, s)),
            (slot(r, close, 1), close, outer, (partner, s)),
            (slot(r, OWN, SPARE), OWN, outer, (onto, s)),
            (slot(r, far, SPARE), far, outer, (onto, s)),
        )
        return remote(flow, r, *table[flow])

    def send(flow, r):
        flow_copy(flow, r).start()

    def arrived(r, side, place):
        remote(0, r, slot(r, side, place), side, place, (mate, s)).wait_recv()

    def signal(semaphore, target):
        pl.semaphore_signal(
            semaphore, inc=1, device_id={"energy": target[0], "slab": target[1]}, device_id_type=MESH
        )

    barrier = pltpu.get_barrier_semaphore()
    upper, lower = layer == 1, layer == 0

    @pl.when(lower)
    def _():
        signal(barrier, (partner, s))

        @pl.when(has_far)
        def _():
            signal(barrier, (mate, across))

        @pl.when(has_onto)
        def _():
            signal(barrier, (onto, s))

        @pl.when(has_behind)
        def _():
            signal(barrier, (behind, s))
            signal(barrier, (behind, s))

    @pl.when(upper)
    def _():
        signal(barrier, (mate, s))
        signal(barrier, (mate + step, s))

        @pl.when(has_onto)
        def _():
            signal(barrier, (mate + onto - a, s))

        @pl.when(has_behind)
        def _():
            signal(barrier, (mate + behind - a, s))
            signal(barrier, (beside, s))

    scalar_copies = [
        pltpu.make_async_copy(source, target, scalar_sem.at[n])
        for n, (source, target) in enumerate(
            ((occ_hbm, occ_ref), (shift_hbm, shift_ref), (near_hbm, near_ref))
        )
    ]
    for copy in scalar_copies:
        copy.start()
    couple_copy = pltpu.make_async_copy(c_ref, couple, couple_sem)
    couple_copy.start()
    own_copies = [
        pltpu.make_async_copy(own_block(r), slot(r, OWN, 1), own_sem.at[r]) for r in range(CHUNKS)
    ]
    for copy in own_copies:
        copy.start()
    @pl.when(lower | has_far)
    def _():
        told = 3 + 3 * (has_onto.astype(jnp.int32) + has_behind.astype(jnp.int32))
        pl.semaphore_wait(barrier, jnp.where(upper, 1, told))

    @pl.when(upper & has_far)
    def _():
        signal(ready_sem, (mate, across))
        for r in range(AHEAD):
            send(2, r)

    @pl.when(lower)
    def _():
        signal(go_sem, (mate, s))

    @pl.when(upper)
    def _():
        pl.semaphore_wait(go_sem, 1)

    for r in range(CHUNKS):
        send(0, r)
        send(1, r)

    def prepare():
        couple_copy.wait()

        def mode_step(m, _):
            for k in range(ks):
                real_t, imag_t = couple[m, 0, k, 0].T, couple[m, 0, k, 1].T
                adjoint = jnp.concatenate(
                    [
                        jnp.concatenate([real_t, -imag_t], axis=1),
                        jnp.concatenate([imag_t, real_t], axis=1),
                    ],
                    axis=0,
                )
                adjoint_high[m, k], adjoint_low[m, k] = halves(adjoint)
            return 0

        lax.fori_loop(0, modes, mode_step, 0)
        for n, group in enumerate(GROUPS):
            first, last = STARTS[group[0]], STARTS[group[-1]] + ROWS[group[-1]]
            for k in range(ks):
                stacked = jnp.concatenate(
                    [
                        couple[m, 0, k, part][:, first:last]
                        for m in range(modes)
                        for part in range(2)
                    ],
                    axis=1,
                )
                high, low = halves(stacked)
                lefts[n][k, :size] = high
                lefts[n][k, size:] = low

    def pass_own(r):
        arrived(r, OWN, mine)

        @pl.when(has_far)
        def _():
            send(3, r)
            if r + AHEAD < CHUNKS:
                send(2, r + AHEAD)

        @pl.when(has_onto)
        def _():
            send(8, r)

    def pass_mates(r):
        @pl.when(has_far)
        def _():
            arrived(r, far, mine)
            send(4, r)

        @pl.when(has_far & has_onto)
        def _():
            send(9, r)

    def pass_far(r):
        @pl.when(has_far)
        def _():
            arrived(r, far, 1)
            send(6, r)

        @pl.when(has_far & has_beside)
        def _():
            send(5, r)

    def pass_close(r):
        @pl.when(has_close)
        def _():
            arrived(r, close, 1)
            send(7, r)

    def gather(r):
        own_copies[r].wait()
        arrived(r, OWN, inner)

        @pl.when(has_behind)
        def _():
            arrived(r, OWN, outer)

        @pl.when(has_far)
        def _():
            arrived(r, far, inner)

        @pl.when(has_far & has_behind)
        def _():
            arrived(r, far, outer)

        @pl.when(has_close)
        def _():
            arrived(r, close, inner)

        @pl.when(has_close & has_beside)
        def _():
            arrived(r, close, outer)

    first_energy = a * energy_count
    top = energies * energy_count

    def multiply(n):
        group = GROUPS[n]
        rows = sum(ROWS[r] for r in group)
        span = modes * 2 * rows

        def k_step(k, _):
            place = jnp.clip(near_ref[0, k] - s + 1, 0, 2)
            for m in range(modes):
                shift = shift_ref[m]
                count = occ_ref[m]
                pieces = []
                for e in range(energy_count):
                    energy = first_energy + e
                    more = jnp.where(energy + shift < top, count + 1.0, 0.0)
                    less = jnp.where(energy - shift >= 0, count, 0.0)
                    above, below = energy_count + e + shift, energy_count + e - shift
                    for r in group:
                        pieces.append(
                            jnp.concatenate(
                                [
                                    more * bufs[r][place, above, part]
                                    + less * bufs[r][place, below, part]
                                    for part in range(2)
                                ],
                                axis=1,
                            )
                        )
                high, low = halves(jnp.concatenate(pieces, axis=0))
                count_rows = energy_count * rows
                first = jnp.dot(
                    jnp.concatenate([high, low], axis=0),
                    adjoint_high[m, k],
                    preferred_element_type=jnp.float32,
                )
                second = jnp.dot(high, adjoint_low[m, k], preferred_element_type=jnp.float32)
                result = first[:count_rows] + first[count_rows:] + second
                for e in range(energy_count):
                    part = result[e * rows : (e + 1) * rows]
                    turned = jnp.concatenate([-part[:, size:], part[:, :size]], axis=1)
                    base = m * 2 * rows
                    columns = slice(e * 2 * size, (e + 1) * 2 * size)
                    for offset, value in ((0, part), (rows, turned)):
                        high_value, low_value = halves(value)
                        middle_high[base + offset : base + offset + rows, columns] = high_value
                        middle_low[base + offset : base + offset + rows, columns] = low_value
            lhs = lefts[n][k]
            both = jnp.dot(lhs, middle_high[:span], preferred_element_type=jnp.float32)
            rest = jnp.dot(lhs[:size], middle_low[:span], preferred_element_type=jnp.float32)
            total[...] += both[:size] + both[size:] + rest
            return 0

        lax.fori_loop(0, ks, k_step, 0)

    @pl.when((layer == 0) & has_far)
    def _():
        pl.semaphore_wait(ready_sem, 1)
        for r in range(AHEAD):
            send(2, r)

    for copy in scalar_copies:
        copy.wait()
    prepare()
    total[...] = jnp.zeros_like(total)

    @pl.when(edge & ~has_behind)
    def _():
        for r in range(CHUNKS):
            for side in range(3):
                for e in range(energy_count):
                    bufs[r][side, energy_count * outer + e] = jnp.zeros((2, ROWS[r], size), jnp.float32)

    pass_own(0)
    pass_own(1)
    pass_mates(0)
    pass_own(2)
    pass_mates(1)
    pass_own(3)
    pass_mates(2)
    pass_mates(3)
    pass_far(0)
    pass_far(1)
    pass_far(2)
    pass_far(3)
    pass_close(0)
    pass_close(1)
    pass_close(2)
    pass_close(3)
    for n, group in enumerate(GROUPS):
        for r in group:
            gather(r)
        multiply(n)
    for e in range(energy_count):
        for part in range(2):
            start = (2 * e + part) * size
            out_ref[e, 0, part] = total[:, start : start + size]

    for r in range(CHUNKS):
        for flows, sent in (
            ((0, 1), None),
            ((2, 3, 4, 6), has_far),
            ((5,), has_far & has_beside),
            ((7,), has_close),
            ((8,), has_onto),
            ((9,), has_far & has_onto),
        ):

            def finish(flows=flows, r=r):
                for flow in flows:
                    flow_copy(flow, r).wait_send()

            if sent is None:
                finish()
            else:
                pl.when(sent)(finish)


def solution(mesh):
    energies, slabs = mesh.shape["energy"], mesh.shape["slab"]

    def shards(green_lesser, coupling, occupation, shifts, neighbours):
        energy_count, _, _, size, _ = green_lesser.shape
        modes, _, ks = coupling.shape[:3]
        bf16, f32 = jnp.bfloat16, jnp.float32
        hbm = pl.BlockSpec(memory_space=pl.ANY)
        spans = [modes * 2 * sum(ROWS[r] for r in group) for group in GROUPS]
        depth = max(spans)
        total = pl.pallas_call(
            functools.partial(kernel, energy_count, energies, slabs),
            out_shape=pltpu.VMEM(green_lesser.shape, f32),
            in_specs=[hbm] * 5,
            out_specs=pl.BlockSpec(memory_space=pltpu.VMEM),
            scratch_shapes=[pltpu.VMEM((3, 4 * energy_count, 2, rows, size), f32) for rows in ROWS]
            + [pltpu.VMEM((ks, 2 * size, span), bf16) for span in spans]
            + [
                pltpu.VMEM(coupling.shape, f32),
                pltpu.VMEM((modes, ks, 2 * size, 2 * size), bf16),
                pltpu.VMEM((modes, ks, 2 * size, 2 * size), bf16),
                pltpu.VMEM((depth, energy_count * 2 * size), bf16),
                pltpu.VMEM((depth, energy_count * 2 * size), bf16),
                pltpu.VMEM((size, energy_count * 2 * size), f32),
                pltpu.SMEM(occupation.shape, f32),
                pltpu.SMEM(shifts.shape, jnp.int32),
                pltpu.SMEM(neighbours.shape, jnp.int32),
                pltpu.SemaphoreType.DMA((10, CHUNKS)),
                pltpu.SemaphoreType.DMA((CHUNKS, 3, 4)),
                pltpu.SemaphoreType.DMA((CHUNKS,)),
                pltpu.SemaphoreType.DMA,
                pltpu.SemaphoreType.DMA((3,)),
                pltpu.SemaphoreType.REGULAR,
                pltpu.SemaphoreType.REGULAR,
            ],
            compiler_params=pltpu.CompilerParams(collective_id=0, has_side_effects=True),
        )(occupation, shifts, neighbours, green_lesser, coupling)
        return total

    return jax.shard_map(
        shards,
        mesh=mesh,
        in_specs=(
            P("energy", "slab", None, None, None),
            P(None, "slab", None, None, None, None),
            P(),
            P(),
            P("slab", None),
        ),
        out_specs=P("energy", "slab", None, None, None),
        check_vma=False,
    )
```

```python
import functools

import jax
import jax.numpy as jnp
from jax import lax
from jax.experimental import pallas as pl
from jax.experimental.pallas import tpu as pltpu
from jax.sharding import PartitionSpec as P

MESH = pl.DeviceIdType.MESH
ROWS = (32, 32, 32, 32)
STARTS = tuple(sum(ROWS[:r]) for r in range(len(ROWS)))
CHUNKS = len(ROWS)
LAG = 1
AHEAD = 4
GROUPS = ((0, 1), (2, 3))
OWN, FAR, CLOSE = range(3)
SPARE = 3


def halves(value):
    high = value.astype(jnp.bfloat16)
    return high, (value - high.astype(jnp.float32)).astype(jnp.bfloat16)


def kernel(energy_count, energies, slabs, occ_hbm, shift_hbm, near_hbm, g_ref, c_ref, out_ref, *scratch):
    bufs, scratch = scratch[: 3 * CHUNKS], scratch[3 * CHUNKS :]
    picked, scratch = scratch[:CHUNKS], scratch[CHUNKS:]
    lefts, scratch = scratch[: len(GROUPS)], scratch[len(GROUPS) :]
    couple, adjoint_high, adjoint_low, middle_high, middle_low, total = scratch[:6]
    occ_ref, shift_ref, near_ref = scratch[6:9]
    send_sem, recv_sem, own_sem, couple_sem, scalar_sem, ready_sem, go_sem = scratch[9:]
    modes, ks, size = c_ref.shape[0], c_ref.shape[2], c_ref.shape[-1]

    a, s = lax.axis_index("energy"), lax.axis_index("slab")
    core, layer = lax.rem(a, 2), lax.rem(lax.div(a, 2), 2)
    step = 2 * core - 1
    partner = a - step
    mate = a + 3 - 2 * lax.rem(a, 4)
    edge = core == layer
    onto, behind = a - 4 * step, a + 4 * step
    has_onto = edge & (onto >= 0) & (onto < energies)
    has_behind = edge & (behind >= 0) & (behind < energies)
    beside = a + step
    has_beside = (beside >= 0) & (beside < energies)
    across = jnp.where(layer == 0, s - 1, s + 1)
    opposite = 2 * s - across
    far_k = 2 * layer
    close_k = 2 - far_k
    has_far = (across >= 0) & (across < slabs)
    has_close = (opposite >= 0) & (opposite < slabs)
    inner, outer = 1 - step, 1 + step
    mine, theirs = jnp.where(edge, SPARE, outer), jnp.where(edge, SPARE, inner)

    def own_block(r):
        return g_ref.at[:, 0, :, pl.ds(STARTS[r], ROWS[r]), :]

    def slot(r, side, place):
        return bufs[3 * r + side].at[pl.ds(energy_count * place, energy_count)]

    def remote(flow, r, source, side, place, target):
        return pltpu.make_async_remote_copy(
            src_ref=source,
            dst_ref=slot(r, side, place),
            send_sem=send_sem.at[flow, r],
            recv_sem=recv_sem.at[r, side, place],
            device_id={"energy": target[0], "slab": target[1]},
            device_id_type=MESH,
        )

    def flow_copy(flow, r):
        own = own_block(r)
        table = (
            (own, OWN, theirs, (mate, s)),
            (own, OWN, outer, (partner, s)),
            (own, FAR, theirs, (mate, across)),
            (slot(r, OWN, mine), FAR, 1, (mate, across)),
            (slot(r, FAR, mine), CLOSE, 1, (mate, s)),
            (slot(r, FAR, 1), CLOSE, inner, (beside, s)),
            (slot(r, FAR, 1), FAR, outer, (partner, s)),
            (slot(r, CLOSE, 1), CLOSE, outer, (partner, s)),
            (slot(r, OWN, SPARE), OWN, outer, (onto, s)),
            (slot(r, FAR, SPARE), FAR, outer, (onto, s)),
        )
        return remote(flow, r, *table[flow])

    def send(flow, r):
        flow_copy(flow, r).start()

    def arrived(r, side, place):
        remote(0, r, slot(r, side, place), side, place, (mate, s)).wait_recv()

    def signal(semaphore, target):
        pl.semaphore_signal(
            semaphore, inc=1, device_id={"energy": target[0], "slab": target[1]}, device_id_type=MESH
        )

    barrier = pltpu.get_barrier_semaphore()
    upper, lower = layer == 1, layer == 0

    @pl.when(lower)
    def _():
        signal(barrier, (partner, s))

        @pl.when(has_far)
        def _():
            signal(barrier, (mate, across))

        @pl.when(has_onto)
        def _():
            signal(barrier, (onto, s))

        @pl.when(has_behind)
        def _():
            signal(barrier, (behind, s))
            signal(barrier, (behind, s))

    @pl.when(upper)
    def _():
        signal(barrier, (mate, s))
        signal(barrier, (mate + step, s))

        @pl.when(has_onto)
        def _():
            signal(barrier, (mate + onto - a, s))

        @pl.when(has_behind)
        def _():
            signal(barrier, (mate + behind - a, s))
            signal(barrier, (beside, s))

    scalar_copies = [
        pltpu.make_async_copy(source, target, scalar_sem.at[n])
        for n, (source, target) in enumerate(
            ((occ_hbm, occ_ref), (shift_hbm, shift_ref), (near_hbm, near_ref))
        )
    ]
    for copy in scalar_copies:
        copy.start()
    couple_copy = pltpu.make_async_copy(c_ref, couple, couple_sem)
    couple_copy.start()
    own_copies = [
        pltpu.make_async_copy(own_block(r), slot(r, OWN, 1), own_sem.at[r]) for r in range(CHUNKS)
    ]
    for copy in own_copies:
        copy.start()
    @pl.when(lower | has_far)
    def _():
        told = 3 + 3 * (has_onto.astype(jnp.int32) + has_behind.astype(jnp.int32))
        pl.semaphore_wait(barrier, jnp.where(upper, 1, told))

    @pl.when(upper & has_far)
    def _():
        signal(ready_sem, (mate, across))
        for r in range(AHEAD):
            send(2, r)

    @pl.when(lower)
    def _():
        signal(go_sem, (mate, s))

    @pl.when(upper)
    def _():
        pl.semaphore_wait(go_sem, 1)

    for r in range(CHUNKS):
        send(0, r)
        send(1, r)

    def prepare():
        couple_copy.wait()

        def mode_step(m, _):
            for k in range(ks):
                real_t, imag_t = couple[m, 0, k, 0].T, couple[m, 0, k, 1].T
                adjoint = jnp.concatenate(
                    [
                        jnp.concatenate([real_t, -imag_t], axis=1),
                        jnp.concatenate([imag_t, real_t], axis=1),
                    ],
                    axis=0,
                )
                adjoint_high[m, k], adjoint_low[m, k] = halves(adjoint)
            return 0

        lax.fori_loop(0, modes, mode_step, 0)
        for n, group in enumerate(GROUPS):
            first, last = STARTS[group[0]], STARTS[group[-1]] + ROWS[group[-1]]
            for k in range(ks):
                stacked = jnp.concatenate(
                    [
                        couple[m, 0, k, part][:, first:last]
                        for m in range(modes)
                        for part in range(2)
                    ],
                    axis=1,
                )
                high, low = halves(stacked)
                lefts[n][k, :size] = high
                lefts[n][k, size:] = low

    def pass_own(r):
        arrived(r, OWN, mine)

        @pl.when(has_far)
        def _():
            send(3, r)
            if r + AHEAD < CHUNKS:
                send(2, r + AHEAD)

        @pl.when(has_onto)
        def _():
            send(8, r)

    def pass_mates(r):
        @pl.when(has_far)
        def _():
            arrived(r, FAR, mine)
            send(4, r)

        @pl.when(has_far & has_onto)
        def _():
            send(9, r)

    def pass_far(r):
        @pl.when(has_far)
        def _():
            arrived(r, FAR, 1)
            send(6, r)

        @pl.when(has_far & has_beside)
        def _():
            send(5, r)

    def pass_close(r):
        @pl.when(has_close)
        def _():
            arrived(r, CLOSE, 1)
            send(7, r)

    def gather_own(r):
        own_copies[r].wait()
        arrived(r, OWN, inner)

        @pl.when(has_behind)
        def _():
            arrived(r, OWN, outer)

    def gather_far(r):
        arrived(r, FAR, inner)

        @pl.when(has_behind)
        def _():
            arrived(r, FAR, outer)

    def gather_close(r):
        arrived(r, CLOSE, inner)

        @pl.when(has_beside)
        def _():
            arrived(r, CLOSE, outer)

    first_energy = a * energy_count
    top = energies * energy_count

    def multiply(n, sources, k):
        group = GROUPS[n]
        rows = sum(ROWS[r] for r in group)
        span = modes * 2 * rows
        for m in range(modes):
            shift = shift_ref[m]
            count = occ_ref[m]
            pieces = []
            for e in range(energy_count):
                energy = first_energy + e
                more = jnp.where(energy + shift < top, count + 1.0, 0.0)
                less = jnp.where(energy - shift >= 0, count, 0.0)
                above, below = energy_count + e + shift, energy_count + e - shift
                for r in group:
                    pieces.append(
                        jnp.concatenate(
                            [
                                more * sources[r][above, part]
                                + less * sources[r][below, part]
                                for part in range(2)
                            ],
                            axis=1,
                        )
                    )
            high, low = halves(jnp.concatenate(pieces, axis=0))
            count_rows = energy_count * rows
            first = jnp.dot(
                jnp.concatenate([high, low], axis=0),
                adjoint_high[m, k],
                preferred_element_type=jnp.float32,
            )
            second = jnp.dot(high, adjoint_low[m, k], preferred_element_type=jnp.float32)
            result = first[:count_rows] + first[count_rows:] + second
            for e in range(energy_count):
                part = result[e * rows : (e + 1) * rows]
                turned = jnp.concatenate([-part[:, size:], part[:, :size]], axis=1)
                base = m * 2 * rows
                columns = slice(e * 2 * size, (e + 1) * 2 * size)
                for offset, value in ((0, part), (rows, turned)):
                    high_value, low_value = halves(value)
                    middle_high[base + offset : base + offset + rows, columns] = high_value
                    middle_low[base + offset : base + offset + rows, columns] = low_value
        lhs = lefts[n][k]
        both = jnp.dot(lhs, middle_high[:span], preferred_element_type=jnp.float32)
        rest = jnp.dot(lhs[:size], middle_low[:span], preferred_element_type=jnp.float32)
        total[...] += both[:size] + both[size:] + rest

    @pl.when((layer == 0) & has_far)
    def _():
        pl.semaphore_wait(ready_sem, 1)
        for r in range(AHEAD):
            send(2, r)

    for copy in scalar_copies:
        copy.wait()
    prepare()
    total[...] = jnp.zeros_like(total)

    @pl.when(edge & ~has_behind)
    def _():
        for r in range(CHUNKS):
            for side in (OWN, FAR, CLOSE):
                for e in range(energy_count):
                    bufs[3 * r + side][energy_count * outer + e] = jnp.zeros((2, ROWS[r], size), jnp.float32)

    for r in range(CHUNKS + LAG):
        if r < CHUNKS:
            pass_own(r)
        if r >= LAG:
            pass_mates(r - LAG)
    def side_of(side):
        return [bufs[3 * r + side] for r in range(CHUNKS)]

    def multiply_far(n):
        @pl.when(has_far)
        def _():
            for r in GROUPS[n]:
                gather_far(r)
            multiply(n, side_of(FAR), far_k)

    def multiply_close(n):
        @pl.when(has_close)
        def _():
            for r in GROUPS[n]:
                gather_close(r)
            multiply(n, side_of(CLOSE), close_k)

    def multiply_own(n):
        for r in GROUPS[n]:
            gather_own(r)

        @pl.when(~(has_far & has_close))
        def _():
            multiply(n, side_of(OWN), jnp.where(has_far, close_k, far_k))

    def multiply_middle(n):
        place = near_ref[0, 1] - s + 1
        for r in GROUPS[n]:
            for energy in range(3 * energy_count):
                own, far, close = (bufs[3 * r + side][energy] for side in (OWN, FAR, CLOSE))
                picked[r][energy] = jnp.where(place == 1, own, jnp.where(place == far_k, far, close))
        multiply(n, picked, 1)

    groups = range(len(GROUPS))
    first = lax.rem(s, 4) == 0
    waiting = first & (layer == 0)

    @pl.when(waiting)
    def _():
        pass_far(0)
        pass_far(1)
        for r in (0, 1):
            pass_close(r)
        multiply_close(0)
        pass_far(2)
        multiply_own(0)
        multiply_far(0)
        pass_far(3)
        for r in (2, 3):
            pass_close(r)
        multiply_middle(0)
        multiply_close(1)
        multiply_own(1)
        multiply_far(1)
        multiply_middle(1)

    @pl.when(~waiting)
    def _():
        for r in range(CHUNKS):
            pass_far(r)
        for r in range(CHUNKS):
            pass_close(r)
        far_last = ~first & (layer == 1)

        @pl.when(far_last)
        def _():
            for n in groups:
                multiply_close(n)

        @pl.when(~far_last)
        def _():
            for n in groups:
                multiply_far(n)

        for n in groups:
            multiply_own(n)
            pl.when(far_last)(functools.partial(multiply_far, n))
            pl.when(~far_last)(functools.partial(multiply_close, n))
            multiply_middle(n)

    for e in range(energy_count):
        for part in range(2):
            start = (2 * e + part) * size
            out_ref[e, 0, part] = total[:, start : start + size]

    for r in range(CHUNKS):
        for flows, sent in (
            ((0, 1), None),
            ((2, 3, 4, 6), has_far),
            ((5,), has_far & has_beside),
            ((7,), has_close),
            ((8,), has_onto),
            ((9,), has_far & has_onto),
        ):

            def finish(flows=flows, r=r):
                for flow in flows:
                    flow_copy(flow, r).wait_send()

            if sent is None:
                finish()
            else:
                pl.when(sent)(finish)


def solution(mesh):
    energies, slabs = mesh.shape["energy"], mesh.shape["slab"]

    def shards(green_lesser, coupling, occupation, shifts, neighbours):
        energy_count, _, _, size, _ = green_lesser.shape
        modes, _, ks = coupling.shape[:3]
        bf16, f32 = jnp.bfloat16, jnp.float32
        hbm = pl.BlockSpec(memory_space=pl.ANY)
        spans = [modes * 2 * sum(ROWS[r] for r in group) for group in GROUPS]
        depth = max(spans)
        total = pl.pallas_call(
            functools.partial(kernel, energy_count, energies, slabs),
            out_shape=pltpu.VMEM(green_lesser.shape, f32),
            in_specs=[hbm] * 5,
            out_specs=pl.BlockSpec(memory_space=pltpu.VMEM),
            scratch_shapes=[
                pltpu.VMEM((4 * energy_count, 2, rows, size), f32) for rows in ROWS for _ in range(3)
            ]
            + [pltpu.VMEM((3 * energy_count, 2, rows, size), f32) for rows in ROWS]
            + [pltpu.VMEM((ks, 2 * size, span), bf16) for span in spans]
            + [
                pltpu.VMEM(coupling.shape, f32),
                pltpu.VMEM((modes, ks, 2 * size, 2 * size), bf16),
                pltpu.VMEM((modes, ks, 2 * size, 2 * size), bf16),
                pltpu.VMEM((depth, energy_count * 2 * size), bf16),
                pltpu.VMEM((depth, energy_count * 2 * size), bf16),
                pltpu.VMEM((size, energy_count * 2 * size), f32),
                pltpu.SMEM(occupation.shape, f32),
                pltpu.SMEM(shifts.shape, jnp.int32),
                pltpu.SMEM(neighbours.shape, jnp.int32),
                pltpu.SemaphoreType.DMA((10, CHUNKS)),
                pltpu.SemaphoreType.DMA((CHUNKS, 3, 4)),
                pltpu.SemaphoreType.DMA((CHUNKS,)),
                pltpu.SemaphoreType.DMA,
                pltpu.SemaphoreType.DMA((3,)),
                pltpu.SemaphoreType.REGULAR,
                pltpu.SemaphoreType.REGULAR,
            ],
            compiler_params=pltpu.CompilerParams(collective_id=0, has_side_effects=True),
        )(occupation, shifts, neighbours, green_lesser, coupling)
        return total

    return jax.shard_map(
        shards,
        mesh=mesh,
        in_specs=(
            P("energy", "slab", None, None, None),
            P(None, "slab", None, None, None, None),
            P(),
            P(),
            P("slab", None),
        ),
        out_specs=P("energy", "slab", None, None, None),
        check_vma=False,
    )
```

```python
import functools

import jax
import jax.numpy as jnp
from jax import lax
from jax.experimental import pallas as pl
from jax.experimental.pallas import tpu as pltpu
from jax.sharding import PartitionSpec as P

MESH = pl.DeviceIdType.MESH
ROWS = (32, 32, 32, 32)
STARTS = tuple(sum(ROWS[:r]) for r in range(len(ROWS)))
CHUNKS = len(ROWS)
LAG = 1
AHEAD = 4
GROUPS = ((0, 1), (2, 3))
OWN, FAR, CLOSE = range(3)
SPARE = 3


def halves(value):
    high = value.astype(jnp.bfloat16)
    return high, (value - high.astype(jnp.float32)).astype(jnp.bfloat16)


def kernel(energy_count, energies, slabs, occ_hbm, shift_hbm, near_hbm, g_ref, c_ref, out_ref, *scratch):
    bufs, scratch = scratch[: 3 * CHUNKS], scratch[3 * CHUNKS :]
    picked, scratch = scratch[:CHUNKS], scratch[CHUNKS:]
    lefts, scratch = scratch[: len(GROUPS)], scratch[len(GROUPS) :]
    couple, adjoint_high, adjoint_low, middle_high, middle_low, total = scratch[:6]
    occ_ref, shift_ref, near_ref = scratch[6:9]
    send_sem, recv_sem, own_sem, couple_sem, scalar_sem, ready_sem, go_sem = scratch[9:]
    modes, ks, size = c_ref.shape[0], c_ref.shape[2], c_ref.shape[-1]

    a, s = lax.axis_index("energy"), lax.axis_index("slab")
    core, layer = lax.rem(a, 2), lax.rem(lax.div(a, 2), 2)
    step = 2 * core - 1
    partner = a - step
    mate = a + 3 - 2 * lax.rem(a, 4)
    edge = core == layer
    onto, behind = a - 4 * step, a + 4 * step
    has_onto = edge & (onto >= 0) & (onto < energies)
    has_behind = edge & (behind >= 0) & (behind < energies)
    beside = a + step
    has_beside = (beside >= 0) & (beside < energies)
    across = jnp.where(layer == 0, s - 1, s + 1)
    opposite = 2 * s - across
    far_k = 2 * layer
    close_k = 2 - far_k
    has_far = (across >= 0) & (across < slabs)
    has_close = (opposite >= 0) & (opposite < slabs)
    inner, outer = 1 - step, 1 + step
    mine, theirs = jnp.where(edge, SPARE, outer), jnp.where(edge, SPARE, inner)

    def own_block(r):
        return g_ref.at[:, 0, :, pl.ds(STARTS[r], ROWS[r]), :]

    def slot(r, side, place):
        return bufs[3 * r + side].at[pl.ds(energy_count * place, energy_count)]

    def remote(flow, r, source, side, place, target):
        return pltpu.make_async_remote_copy(
            src_ref=source,
            dst_ref=slot(r, side, place),
            send_sem=send_sem.at[flow, r],
            recv_sem=recv_sem.at[r, side, place],
            device_id={"energy": target[0], "slab": target[1]},
            device_id_type=MESH,
        )

    def flow_copy(flow, r):
        own = own_block(r)
        table = (
            (own, OWN, theirs, (mate, s)),
            (own, OWN, outer, (partner, s)),
            (own, FAR, theirs, (mate, across)),
            (slot(r, OWN, mine), FAR, 1, (mate, across)),
            (slot(r, FAR, mine), CLOSE, 1, (mate, s)),
            (slot(r, FAR, 1), CLOSE, inner, (beside, s)),
            (slot(r, FAR, 1), FAR, outer, (partner, s)),
            (slot(r, CLOSE, 1), CLOSE, outer, (partner, s)),
            (slot(r, OWN, SPARE), OWN, outer, (onto, s)),
            (slot(r, FAR, SPARE), FAR, outer, (onto, s)),
        )
        return remote(flow, r, *table[flow])

    def send(flow, r):
        flow_copy(flow, r).start()

    def arrived(r, side, place):
        remote(0, r, slot(r, side, place), side, place, (mate, s)).wait_recv()

    def signal(semaphore, target):
        pl.semaphore_signal(
            semaphore, inc=1, device_id={"energy": target[0], "slab": target[1]}, device_id_type=MESH
        )

    barrier = pltpu.get_barrier_semaphore()
    upper, lower = layer == 1, layer == 0

    @pl.when(lower)
    def _():
        signal(barrier, (partner, s))

        @pl.when(has_far)
        def _():
            signal(barrier, (mate, across))

        @pl.when(has_onto)
        def _():
            signal(barrier, (onto, s))

        @pl.when(has_behind)
        def _():
            signal(barrier, (behind, s))
            signal(barrier, (behind, s))

    @pl.when(upper)
    def _():
        signal(barrier, (mate, s))
        signal(barrier, (mate + step, s))

        @pl.when(has_onto)
        def _():
            signal(barrier, (mate + onto - a, s))

        @pl.when(has_behind)
        def _():
            signal(barrier, (mate + behind - a, s))
            signal(barrier, (beside, s))

    @pl.when(lower | has_far)
    def _():
        told = 3 + 3 * (has_onto.astype(jnp.int32) + has_behind.astype(jnp.int32))
        pl.semaphore_wait(barrier, jnp.where(upper, 1, told))

    @pl.when(upper & has_far)
    def _():
        signal(ready_sem, (mate, across))
        for r in range(AHEAD):
            send(2, r)

    scalar_copies = [
        pltpu.make_async_copy(source, target, scalar_sem.at[n])
        for n, (source, target) in enumerate(
            ((occ_hbm, occ_ref), (shift_hbm, shift_ref), (near_hbm, near_ref))
        )
    ]
    for copy in scalar_copies:
        copy.start()
    couple_copy = pltpu.make_async_copy(c_ref, couple, couple_sem)
    couple_copy.start()
    own_copies = [
        pltpu.make_async_copy(own_block(r), slot(r, OWN, 1), own_sem.at[r]) for r in range(CHUNKS)
    ]
    for copy in own_copies:
        copy.start()
    @pl.when(lower)
    def _():
        signal(go_sem, (mate, s))

    @pl.when(upper)
    def _():
        pl.semaphore_wait(go_sem, 1)

    for r in range(CHUNKS):
        send(0, r)
        send(1, r)

    def prepare():
        couple_copy.wait()

        def mode_step(m, _):
            for k in range(ks):
                real_t, imag_t = couple[m, 0, k, 0].T, couple[m, 0, k, 1].T
                adjoint = jnp.concatenate(
                    [
                        jnp.concatenate([real_t, -imag_t], axis=1),
                        jnp.concatenate([imag_t, real_t], axis=1),
                    ],
                    axis=0,
                )
                adjoint_high[m, k], adjoint_low[m, k] = halves(adjoint)
            return 0

        lax.fori_loop(0, modes, mode_step, 0)
        for n, group in enumerate(GROUPS):
            first, last = STARTS[group[0]], STARTS[group[-1]] + ROWS[group[-1]]
            for k in range(ks):
                stacked = jnp.concatenate(
                    [
                        couple[m, 0, k, part][:, first:last]
                        for m in range(modes)
                        for part in range(2)
                    ],
                    axis=1,
                )
                high, low = halves(stacked)
                lefts[n][k, :size] = high
                lefts[n][k, size:] = low

    def pass_own(r):
        arrived(r, OWN, mine)

        @pl.when(has_far)
        def _():
            send(3, r)
            if r + AHEAD < CHUNKS:
                send(2, r + AHEAD)

        @pl.when(has_onto)
        def _():
            send(8, r)

    def pass_mates(r):
        @pl.when(has_far)
        def _():
            arrived(r, FAR, mine)
            send(4, r)

        @pl.when(has_far & has_onto)
        def _():
            send(9, r)

    def pass_far(r):
        @pl.when(has_far)
        def _():
            arrived(r, FAR, 1)
            send(6, r)

        @pl.when(has_far & has_beside)
        def _():
            send(5, r)

    def pass_close(r):
        @pl.when(has_close)
        def _():
            arrived(r, CLOSE, 1)
            send(7, r)

    def gather_own(r):
        own_copies[r].wait()
        arrived(r, OWN, inner)

        @pl.when(has_behind)
        def _():
            arrived(r, OWN, outer)

    def gather_far(r):
        arrived(r, FAR, inner)

        @pl.when(has_behind)
        def _():
            arrived(r, FAR, outer)

    def gather_close(r):
        arrived(r, CLOSE, inner)

        @pl.when(has_beside)
        def _():
            arrived(r, CLOSE, outer)

    first_energy = a * energy_count
    top = energies * energy_count

    def multiply(n, sources, k):
        group = GROUPS[n]
        rows = sum(ROWS[r] for r in group)
        span = modes * 2 * rows
        for m in range(modes):
            shift = shift_ref[m]
            count = occ_ref[m]
            pieces = []
            for e in range(energy_count):
                energy = first_energy + e
                more = jnp.where(energy + shift < top, count + 1.0, 0.0)
                less = jnp.where(energy - shift >= 0, count, 0.0)
                above, below = energy_count + e + shift, energy_count + e - shift
                for r in group:
                    pieces.append(
                        jnp.concatenate(
                            [
                                more * sources[r][above, part]
                                + less * sources[r][below, part]
                                for part in range(2)
                            ],
                            axis=1,
                        )
                    )
            high, low = halves(jnp.concatenate(pieces, axis=0))
            count_rows = energy_count * rows
            first = jnp.dot(
                jnp.concatenate([high, low], axis=0),
                adjoint_high[m, k],
                preferred_element_type=jnp.float32,
            )
            second = jnp.dot(high, adjoint_low[m, k], preferred_element_type=jnp.float32)
            result = first[:count_rows] + first[count_rows:] + second
            for e in range(energy_count):
                part = result[e * rows : (e + 1) * rows]
                turned = jnp.concatenate([-part[:, size:], part[:, :size]], axis=1)
                base = m * 2 * rows
                columns = slice(e * 2 * size, (e + 1) * 2 * size)
                for offset, value in ((0, part), (rows, turned)):
                    high_value, low_value = halves(value)
                    middle_high[base + offset : base + offset + rows, columns] = high_value
                    middle_low[base + offset : base + offset + rows, columns] = low_value
        lhs = lefts[n][k]
        both = jnp.dot(lhs, middle_high[:span], preferred_element_type=jnp.float32)
        rest = jnp.dot(lhs[:size], middle_low[:span], preferred_element_type=jnp.float32)
        total[...] += both[:size] + both[size:] + rest

    @pl.when((layer == 0) & has_far)
    def _():
        pl.semaphore_wait(ready_sem, 1)
        for r in range(AHEAD):
            send(2, r)

    for copy in scalar_copies:
        copy.wait()
    prepare()
    total[...] = jnp.zeros_like(total)

    @pl.when(edge & ~has_behind)
    def _():
        for r in range(CHUNKS):
            for side in (OWN, FAR, CLOSE):
                for e in range(energy_count):
                    bufs[3 * r + side][energy_count * outer + e] = jnp.zeros((2, ROWS[r], size), jnp.float32)

    for r in range(CHUNKS + LAG):
        if r < CHUNKS:
            pass_own(r)
        if r >= LAG:
            pass_mates(r - LAG)
    def side_of(side):
        return [bufs[3 * r + side] for r in range(CHUNKS)]

    def multiply_far(n):
        @pl.when(has_far)
        def _():
            for r in GROUPS[n]:
                gather_far(r)
            multiply(n, side_of(FAR), far_k)

    def multiply_close(n):
        @pl.when(has_close)
        def _():
            for r in GROUPS[n]:
                gather_close(r)
            multiply(n, side_of(CLOSE), close_k)

    def multiply_own(n):
        for r in GROUPS[n]:
            gather_own(r)

        @pl.when(~(has_far & has_close))
        def _():
            multiply(n, side_of(OWN), jnp.where(has_far, close_k, far_k))

    def multiply_middle(n):
        place = near_ref[0, 1] - s + 1
        for r in GROUPS[n]:
            for energy in range(3 * energy_count):
                own, far, close = (bufs[3 * r + side][energy] for side in (OWN, FAR, CLOSE))
                picked[r][energy] = jnp.where(place == 1, own, jnp.where(place == far_k, far, close))
        multiply(n, picked, 1)

    groups = range(len(GROUPS))
    first = lax.rem(s, 4) == 0
    waiting = first & (layer == 0)

    @pl.when(waiting)
    def _():
        pass_far(0)
        pass_far(1)
        for r in (0, 1):
            pass_close(r)
        multiply_close(0)
        pass_far(2)
        multiply_own(0)
        multiply_far(0)
        pass_far(3)
        for r in (2, 3):
            pass_close(r)
        multiply_middle(0)
        multiply_close(1)
        multiply_own(1)
        multiply_far(1)
        multiply_middle(1)

    @pl.when(~waiting)
    def _():
        for r in range(CHUNKS):
            pass_far(r)
        for r in range(CHUNKS):
            pass_close(r)
        far_last = ~first & (layer == 1)

        @pl.when(far_last)
        def _():
            for n in groups:
                multiply_close(n)

        @pl.when(~far_last)
        def _():
            for n in groups:
                multiply_far(n)

        for n in groups:
            multiply_own(n)
            pl.when(far_last)(functools.partial(multiply_far, n))
            pl.when(~far_last)(functools.partial(multiply_close, n))
            multiply_middle(n)

    for e in range(energy_count):
        for part in range(2):
            start = (2 * e + part) * size
            out_ref[e, 0, part] = total[:, start : start + size]

    for r in range(CHUNKS):
        for flows, sent in (
            ((0, 1), None),
            ((2, 3, 4, 6), has_far),
            ((5,), has_far & has_beside),
            ((7,), has_close),
            ((8,), has_onto),
            ((9,), has_far & has_onto),
        ):

            def finish(flows=flows, r=r):
                for flow in flows:
                    flow_copy(flow, r).wait_send()

            if sent is None:
                finish()
            else:
                pl.when(sent)(finish)


def solution(mesh):
    energies, slabs = mesh.shape["energy"], mesh.shape["slab"]

    def shards(green_lesser, coupling, occupation, shifts, neighbours):
        energy_count, _, _, size, _ = green_lesser.shape
        modes, _, ks = coupling.shape[:3]
        bf16, f32 = jnp.bfloat16, jnp.float32
        hbm = pl.BlockSpec(memory_space=pl.ANY)
        spans = [modes * 2 * sum(ROWS[r] for r in group) for group in GROUPS]
        depth = max(spans)
        total = pl.pallas_call(
            functools.partial(kernel, energy_count, energies, slabs),
            out_shape=pltpu.VMEM(green_lesser.shape, f32),
            in_specs=[hbm] * 5,
            out_specs=pl.BlockSpec(memory_space=pltpu.VMEM),
            scratch_shapes=[
                pltpu.VMEM((4 * energy_count, 2, rows, size), f32) for rows in ROWS for _ in range(3)
            ]
            + [pltpu.VMEM((3 * energy_count, 2, rows, size), f32) for rows in ROWS]
            + [pltpu.VMEM((ks, 2 * size, span), bf16) for span in spans]
            + [
                pltpu.VMEM(coupling.shape, f32),
                pltpu.VMEM((modes, ks, 2 * size, 2 * size), bf16),
                pltpu.VMEM((modes, ks, 2 * size, 2 * size), bf16),
                pltpu.VMEM((depth, energy_count * 2 * size), bf16),
                pltpu.VMEM((depth, energy_count * 2 * size), bf16),
                pltpu.VMEM((size, energy_count * 2 * size), f32),
                pltpu.SMEM(occupation.shape, f32),
                pltpu.SMEM(shifts.shape, jnp.int32),
                pltpu.SMEM(neighbours.shape, jnp.int32),
                pltpu.SemaphoreType.DMA((10, CHUNKS)),
                pltpu.SemaphoreType.DMA((CHUNKS, 3, 4)),
                pltpu.SemaphoreType.DMA((CHUNKS,)),
                pltpu.SemaphoreType.DMA,
                pltpu.SemaphoreType.DMA((3,)),
                pltpu.SemaphoreType.REGULAR,
                pltpu.SemaphoreType.REGULAR,
            ],
            compiler_params=pltpu.CompilerParams(collective_id=0, has_side_effects=True),
        )(occupation, shifts, neighbours, green_lesser, coupling)
        return total

    return jax.shard_map(
        shards,
        mesh=mesh,
        in_specs=(
            P("energy", "slab", None, None, None),
            P(None, "slab", None, None, None, None),
            P(),
            P(),
            P("slab", None),
        ),
        out_specs=P("energy", "slab", None, None, None),
        check_vma=False,
    )
```
